256 devices in a mesh: tm: 32 (over z, x), rows: 8 (over y, core).
Axes of the slice: x: 4, y: 4, z: 8, core: 2. Of those that a mesh axis runs over, the one named last changes fastest.
Arguments:
- x_start: float32 [1, 16, 128, 128], P(None, None, 'rows'), may hold values from -6 to 6
- noise: float32 [32, 1, 16, 128, 128], P('tm', None, None, 'rows'), may hold values from -6 to 6
- fresh: float32 [5, 1, 16, 128, 128], P(None, None, None, 'rows'), may hold values from -6 to 6
- sched: int32 [38], replicated, may hold values from 888 to 999, as said below
- conv_in: bfloat16 [3, 3, 192, 16], replicated, may hold values from -0.5 to 0.5
- conv_mid: bfloat16 [3, 3, 192, 192], replicated, may hold values from -0.15625 to 0.15625
- conv_out: bfloat16 [3, 3, 16, 192], replicated, may hold values from -0.15625 to 0.15625
- time_weight: bfloat16 [192, 192], replicated, may hold values from -0.4375 to 0.4375
Outputs:
- trajectory: float32 [2, 32, 1, 16, 128, 128], P(None, 'tm', None, None, 'rows')
The draws below stay inside these ranges and needn't reach their ends.
Inputs may be any that keep to these rules, and one draw needn't show every extreme that they name: sched[0] = 999 and each entry is 1 to 3 below the one before it.
All inputs are finite; a program needn't handle non-finite values.
Results may differ from the reference program's by a relative error of at most 0.00055.
Values may be sent and summed in bfloat16 or wider, within the bound.
No kernel may reach another device: no remote copies, remote signals or barrier semaphores. Data moves between devices by JAX's collectives and lax.ppermute only.
A program may use at most 64 MiB of HBM per device.

```python
import jax
import jax.numpy as jnp
from jax import lax

LAT_CH = 16
HIDDEN_SIZE = 192
COLS = 128
FRAMES = 1
STEPS = 1000
SWEEPS = 2
RETIRE = 5
ROUNDS = 2
WINDOW = 32
HEIGHT = 128
SPAN = 38


def draw_sched(key, part):
    strides = jax.random.randint(key, (SPAN,), 1, 4)
    strides = jnp.where(jnp.arange(SPAN) == 0, 0, strides)
    return (STEPS - 1 - jnp.cumsum(strides)).astype(jnp.int32)


def shard_levels(key, shape, pieces, least, top_value):
    def one(axis_at, parts):
        heights = jax.random.uniform(jax.random.fold_in(jax.random.fold_in(key, 6), axis_at), (parts,), jnp.float32, least / len(pieces), top_value / len(pieces))
        return jnp.repeat(jnp.exp(heights), shape[axis_at] // parts).reshape((-1,) + (1,) * (len(shape) - axis_at - 1))

    gain = one(*pieces[0])
    for cut in pieces[1:]:
        gain = gain * one(*cut)
    return gain


def centred(stream_key, extent, deviation, most, split=(), kind=jnp.bfloat16):
    array = deviation * jax.random.normal(stream_key, extent, jnp.float32)
    if split:
        array = array * shard_levels(stream_key, extent, split, -0.22, 0.18)
    return jnp.clip(array, -most, most).astype(kind)


def setup_inputs(seed: int = 0) -> dict:
    arg_keys = jax.random.split(jax.random.key(seed), 9)
    x_start = centred(arg_keys[0], (FRAMES, LAT_CH, HEIGHT, COLS), 1.0, 6.0, ((2, 8),), jnp.float32)
    noise = centred(arg_keys[1], (WINDOW, FRAMES, LAT_CH, HEIGHT, COLS), 1.0, 6.0, ((0, 32), (3, 8)), jnp.float32)
    fresh = centred(arg_keys[2], ((ROUNDS - 1) * RETIRE, FRAMES, LAT_CH, HEIGHT, COLS), 1.0, 6.0, ((3, 8),), jnp.float32)
    sched = draw_sched(jax.random.fold_in(arg_keys[8], 71), 0)
    conv_in = centred(arg_keys[4], (3, 3, HIDDEN_SIZE, LAT_CH), (9 * LAT_CH) ** -0.5, 0.5)
    conv_mid = centred(arg_keys[5], (3, 3, HIDDEN_SIZE, HIDDEN_SIZE), (9 * HIDDEN_SIZE) ** -0.5, 0.15625)
    conv_out = centred(arg_keys[6], (3, 3, LAT_CH, HIDDEN_SIZE), (9 * HIDDEN_SIZE) ** -0.5, 0.15625)
    time_weight = centred(arg_keys[7], (HIDDEN_SIZE, HIDDEN_SIZE), HIDDEN_SIZE ** -0.5, 0.4375)
    return {"x_start": x_start, "noise": noise, "fresh": fresh, "sched": sched, "conv_in": conv_in, "conv_mid": conv_mid, "conv_out": conv_out, "time_weight": time_weight}


log_base = 9.210340371976184

def plan_table(total_steps):
    positions = jnp.arange(total_steps).astype(jnp.float32)
    betas = 0.0001 + (0.02 - 0.0001) * positions / (total_steps - 1)
    return jnp.cumsum(jnp.log(1.0 - betas))

def coefficients(log_now, log_next):
    retained = jnp.exp(log_now - log_next)
    bar_now = jnp.exp(log_now)
    bar_next = jnp.exp(log_next)
    keep = 1.0 / jnp.sqrt(retained) - 1.0
    predict = -(1.0 - retained) / (jnp.sqrt(1.0 - bar_now) * jnp.sqrt(retained))
    spread = jnp.sqrt((1.0 - bar_next) / (1.0 - bar_now) * (1.0 - retained))
    return (keep, predict, spread)

def time_features(now_value, width):
    half = width // 2
    freqs = jnp.exp(-log_base * jnp.arange(half).astype(jnp.float32) / half)
    angles = now_value[..., None] * freqs
    return jnp.concatenate([jnp.sin(angles), jnp.cos(angles)], axis=-1)

def convolve_full(values, weight):
    widened = jnp.pad(values, ((0, 0), (0, 0), (0, 0), (1, 1), (1, 1)))
    height, columns = (values.shape[3], values.shape[4])
    running = jnp.zeros(values.shape[:2] + (weight.shape[2], height, columns), jnp.float32)
    for row_tap in range(3):
        for col_tap in range(3):
            shifted = widened[:, :, :, row_tap:row_tap + height, col_tap:col_tap + columns]
            running = running + jnp.einsum('oc,sfcrw->sforw', weight[row_tap, col_tap].astype(jnp.float32), shifted, precision=lax.Precision.HIGHEST)
    return running

def rounded(values):
    return lax.optimization_barrier(values.astype(jnp.bfloat16)).astype(jnp.float32)

def network(state, embedding, conv_in, conv_mid, conv_out):
    latent = rounded(state)
    first = convolve_full(latent, conv_in) + embedding[:, None, :, None, None]
    first = rounded(jax.nn.silu(first))
    second = rounded(jax.nn.silu(convolve_full(first, conv_mid)))
    return convolve_full(second, conv_out)

def reference(x_start, noise, fresh, sched, conv_in, conv_mid, conv_out, time_weight):
    table = plan_table(STEPS)
    state = jnp.broadcast_to(x_start[None], (WINDOW,) + x_start.shape)
    noise_now = noise
    base_state = x_start
    snapshots = []
    for round_index in range(ROUNDS):
        offset = RETIRE * round_index
        now_steps = sched[offset:offset + WINDOW]
        next_steps = sched[offset + 1:offset + WINDOW + 1]
        keep, predict, spread = coefficients(table[now_steps], table[next_steps])
        features = time_features(now_steps.astype(jnp.float32), HIDDEN_SIZE)
        embedding = jnp.dot(features, time_weight.astype(jnp.float32), precision=lax.Precision.HIGHEST)
        for sweep_index in range(SWEEPS):
            predicted = network(state, embedding, conv_in, conv_mid, conv_out)
            change = keep[:, None, None, None, None] * state + predict[:, None, None, None, None] * predicted + spread[:, None, None, None, None] * noise_now
            running = jnp.cumsum(change, axis=0)
            prior = jnp.concatenate([jnp.zeros_like(change[:1]), running[:-1]], axis=0)
            state = base_state[None] + prior
        snapshots.append(state)
        if round_index + 1 < ROUNDS:
            state = jnp.concatenate([state[RETIRE:], state[WINDOW - RETIRE:]], axis=0)
            noise_now = jnp.concatenate([noise_now[RETIRE:], fresh[round_index * RETIRE:(round_index + 1) * RETIRE]], axis=0)
            base_state = state[0]
    return jnp.stack(snapshots)
```

```python
import functools
import jax
import jax.numpy as jnp
from jax import lax
from jax.experimental import pallas as pl
from jax.experimental.pallas import tpu as pltpu
from jax.sharding import PartitionSpec as P

STEPS = 1000
RETIRE = 5
SLOTS = 32
CH = 16
HID = 192
ROWS = 4
COLS = 16
STEP = 3 * CH
BF = jnp.bfloat16
F32 = jnp.float32


def silu(v):
    half = 0.5 * v
    return half + half * jnp.tanh(half)


def sweep_body(sweep, merge, flags, *refs):
    extra = (9, 6, 3, 0)[sweep]
    out_cols = COLS + 2 * extra
    mid_cols, first_cols = out_cols + 2, out_cols + 4
    lanes = -(-out_cols * CH // 128) * 128
    groups_1 = -(-first_cols // 4)
    if sweep == 0:
        x_ref, z_ref, coef, emb, w_in, w_a, w_b, w_c, w_out, low = refs[:10]
        state_out, up_out, down_out = refs[10:13]
    elif sweep == 1:
        u_ref, s_ref, d_ref, x_ref, z_ref, coef, emb, w_in, w_a, w_b, w_c, w_out, low = refs[:13]
        traj_out, state_out, up_out, down_out = refs[13:17]
    elif sweep == 2:
        u_ref, s_ref, d_ref, z_ref, coef, emb, w_in, w_a, w_b, w_c, w_out, low = refs[:12]
        state_out, up_out, down_out = refs[12:15]
    else:
        u_ref, s_ref, d_ref, old_ref, z_ref, coef, emb, w_in, w_a, w_b, w_c, w_out, low = refs[:13]
        traj_out = refs[13]
    hs, f1, f2 = refs[-3:]
    batch = hs.shape[2]

    for y in range(ROWS + 6):
        if sweep == 0:
            row = x_ref[y].astype(BF)
            row = jnp.concatenate([x_ref[y]] * 2, axis=0).astype(BF)
        elif y < 3:
            row = u_ref[y]
        elif y < 3 + ROWS:
            row = s_ref[y - 3].astype(BF)
        else:
            row = d_ref[y - 3 - ROWS]
        for g in range(groups_1):
            hs[g, y] = row[:, 64 * g : 64 * g + 128]

    def stage_1(g, _):
        lhs = jnp.concatenate([hs[g, a : a + ROWS + 4] for a in range(3)], axis=-1)
        lhs = lhs.reshape((ROWS + 4) * batch, 384)
        for ph in range(3):
            acc = jnp.dot(lhs, w_in[ph], preferred_element_type=F32)
            acc = acc.reshape(ROWS + 4, batch, 256)
            if batch < SLOTS:
                acc = jnp.concatenate([acc] * (SLOTS // batch), axis=1)
            acc = silu(acc + emb[ph][None])
            at = pl.multiple_of(768 * g + 256 * ph, 256)
            f1[:, :, pl.ds(at, 256)] = acc.astype(BF)
        return 0

    lax.fori_loop(0, groups_1, stage_1, 0)

    def clear(ref, ahead, height, top, bottom):
        width = ref.shape[2]

        @pl.when(flags[0] == 1)
        def _():
            ref[:, :, 0 : ahead * HID] = jnp.zeros((height, SLOTS, ahead * HID), BF)

        @pl.when(flags[1] == 1)
        def _():
            ref[:, :, (ahead + COLS) * HID :] = jnp.zeros(
                (height, SLOTS, width - (ahead + COLS) * HID), BF
            )

        @pl.when(flags[2] == 1)
        def _():
            ref[0:top] = jnp.zeros((top, SLOTS, width), BF)

        @pl.when(flags[3] == 1)
        def _():
            ref[height - bottom :] = jnp.zeros((bottom, SLOTS, width), BF)

    clear(f1, extra + 2, ROWS + 4, 2, 2)

    mid_rows = ROWS + 2

    def window(g, off, length):
        at = pl.multiple_of(768 * g + off, 128) if not isinstance(g, int) else 768 * g + off
        part = [f1[a : a + mid_rows, :, pl.ds(at, length)] for a in range(3)]
        return jnp.concatenate(part, axis=-1).reshape(mid_rows * SLOTS, 3 * length)

    def put(g, off, acc):
        at = pl.multiple_of(768 * g + off, 128) if not isinstance(g, int) else 768 * g + off
        size = acc.shape[-1]
        f2[:, :, pl.ds(at, size)] = silu(acc).astype(BF).reshape(mid_rows, SLOTS, size)

    groups_2 = mid_cols // 4
    rows_2 = mid_rows * SLOTS

    def stage_2(gs):
        for off, length, shift, w in ((0, 768, 0, w_a), (128, 896, 256, w_b), (384, 768, 512, w_c)):
            lhs = [window(g, off, length) for g in gs]
            lhs = jnp.concatenate(lhs, axis=0) if len(lhs) > 1 else lhs[0]
            acc = jnp.dot(lhs, w[...].reshape(3 * length, 256), preferred_element_type=F32)
            for i, g in enumerate(gs):
                put(g, shift, acc[i * rows_2 : (i + 1) * rows_2])

    def many(i, _):
        stage_2([i * merge + k for k in range(merge)])
        return 0

    lax.fori_loop(0, groups_2 // merge, many, 0)
    rest = groups_2 % merge
    if rest:
        stage_2([groups_2 - rest + k for k in range(rest)])
    if mid_cols % 4:
        g = groups_2
        acc = jnp.dot(
            window(g, 0, 768), w_a[...].reshape(2304, 256), preferred_element_type=F32
        )
        put(g, 0, acc)
        w = jnp.concatenate([w_b[a, 0:640, 0:128] for a in range(3)], axis=0)
        put(g, 256, jnp.dot(window(g, 128, 640), w, preferred_element_type=F32))
    clear(f2, extra + 1, mid_rows, 1, 1)

    full = out_cols // 8
    lhs = [
        jnp.concatenate([f2[a : a + ROWS, :, 1536 * n : 1536 * n + 1920] for a in range(3)], axis=-1)
        .reshape(ROWS * SLOTS, 5760)
        for n in range(full)
    ]
    lhs = jnp.concatenate(lhs, axis=0)
    acc = jnp.dot(lhs, w_out[...].reshape(5760, 128), preferred_element_type=F32)
    acc = acc.reshape(full, ROWS, SLOTS, 128)
    pieces = [acc[n] for n in range(full)]
    left = out_cols - 8 * full
    if left:
        k = (left + 2) * HID
        at = 1536 * full
        lhs = jnp.concatenate([f2[a : a + ROWS, :, at : at + k] for a in range(3)], axis=-1)
        w = jnp.concatenate([w_out[a, 0:k] for a in range(3)], axis=0)
        acc = jnp.dot(lhs.reshape(ROWS * SLOTS, 3 * k), w, preferred_element_type=F32)
        pieces.append(acc.reshape(ROWS, SLOTS, 128))
    predicted = jnp.concatenate(pieces, axis=-1)

    keep = coef[0][:, 0:1]
    predict = coef[1][:, 0:1]
    spread = coef[2][:, 0:1]
    z_at = STEP if sweep in (1, 3) else 0
    where = lax.broadcasted_iota(jnp.int32, (1, lanes), 1)
    low_lane = jnp.where(flags[0] == 1, extra * CH, 0)
    high_lane = jnp.where(flags[1] == 1, (extra + COLS) * CH, lanes)
    inside = jnp.where((where >= low_lane) & (where < high_lane), 1.0, 0.0).astype(F32)
    changes = []
    for y in range(ROWS):
        if sweep == 0:
            now = jnp.concatenate([x_ref[y + 3, :, STEP : STEP + lanes]] * 4, axis=0)
        else:
            now = s_ref[y, :, STEP : STEP + lanes]
        z = z_ref[y, :, z_at : z_at + lanes]
        changes.append(keep * now + predict * predicted[y] + spread * z)
    change = jnp.concatenate(changes, axis=-1)
    total = jnp.dot(low[...], change, preferred_element_type=F32, precision=lax.Precision.HIGHEST)
    for y in range(ROWS):
        if sweep == 0:
            base = x_ref[y + 3, 0:1, STEP : STEP + lanes]
        elif sweep == 1:
            base = x_ref[y + 3, 0:1, 2 * STEP : 2 * STEP + lanes]
        elif sweep == 2:
            base = s_ref[y, 0:1, STEP : STEP + lanes]
        else:
            base = old_ref[y, 0:1, 2 * STEP : 2 * STEP + lanes]
        state = base + total[0:SLOTS, y * lanes : (y + 1) * lanes]
        if sweep == 1:
            traj_out[y] = state[:, 2 * STEP : 2 * STEP + COLS * CH]
            state = base + total[SLOTS:, y * lanes : (y + 1) * lanes]
        if sweep == 3:
            traj_out[y] = state
        else:
            state = state * inside
            state_out[y] = state
            if y < 3:
                up_out[y] = state.astype(BF)
            if y > 0:
                down_out[y - 1] = state.astype(BF)


def sweep_call(sweep, merge, flags, args):
    extra = (9, 6, 3, 0)[sweep]
    out_cols = COLS + 2 * extra
    lanes = -(-out_cols * CH // 128) * 128
    groups_1 = -(-(out_cols + 4) // 4)
    groups_2 = (out_cols + 2) // 4
    f1_lanes = max(groups_1 * 768, (groups_2 - 1) * 768 + 1152)
    shapes = []
    if sweep in (1, 3):
        shapes.append(jax.ShapeDtypeStruct((ROWS, SLOTS, COLS * CH), F32))
    if sweep < 3:
        shapes.append(jax.ShapeDtypeStruct((ROWS, SLOTS, lanes), F32))
        shapes += [jax.ShapeDtypeStruct((3, SLOTS, lanes), BF)] * 2
    vmem = pl.BlockSpec(memory_space=pltpu.VMEM)
    out = pl.pallas_call(
        functools.partial(sweep_body, sweep, merge),
        out_shape=tuple(shapes),
        in_specs=[pl.BlockSpec(memory_space=pltpu.SMEM)] + [vmem] * len(args),
        out_specs=tuple([vmem] * len(shapes)),
        scratch_shapes=[
            pltpu.VMEM((groups_1, ROWS + 6, 16 if sweep == 0 else SLOTS, 128), BF),
            pltpu.VMEM((ROWS + 4, SLOTS, f1_lanes), BF),
            pltpu.VMEM((ROWS + 2, SLOTS, (out_cols + 2) * HID), BF),
        ],
        name=f"sweep{sweep}",
    )(flags, *args)
    return out


def plan_values(sched, time_weight, hidden):
    count = sched.shape[0] - 1
    step = jnp.arange(STEPS)
    betas = 0.0001 + (0.02 - 0.0001) * step.astype(F32) / (STEPS - 1)
    logs = jnp.log(1.0 - betas)[None]
    now, after = sched[:count, None], sched[1:, None]
    log_now = jnp.sum(jnp.where(step[None] <= now, logs, 0.0), axis=1)
    log_after = jnp.sum(jnp.where(step[None] <= after, logs, 0.0), axis=1)
    between = (step[None] <= now) & (step[None] > after)
    retained = jnp.exp(jnp.sum(jnp.where(between, logs, 0.0), axis=1))
    bar_now, bar_after = jnp.exp(log_now), jnp.exp(log_after)
    keep = 1.0 / jnp.sqrt(retained) - 1.0
    predict = -(1.0 - retained) / (jnp.sqrt(1.0 - bar_now) * jnp.sqrt(retained))
    spread = jnp.sqrt((1.0 - bar_after) / (1.0 - bar_now) * (1.0 - retained))
    half = hidden // 2
    freqs = jnp.exp(-9.210340371976184 * jnp.arange(half).astype(F32) / half)
    angles = now.astype(F32) * freqs
    features = jnp.concatenate([jnp.sin(angles), jnp.cos(angles)], axis=-1)
    embedding = jnp.dot(features, time_weight.astype(F32), precision=lax.Precision.HIGHEST)
    return jnp.stack([keep, predict, spread]), embedding


def banded_weights(conv_in, conv_mid, conv_out):
    w = conv_in.transpose(0, 1, 3, 2)
    w_in = jnp.stack([jnp.pad(w, ((0, 0), (p, 5 - p), (0, 0), (0, 0))) for p in range(4)], axis=3)
    w_in = w_in.reshape(3 * 8 * CH, 3, 256).transpose(1, 0, 2)
    w = conv_mid.transpose(0, 1, 3, 2)
    w = jnp.stack([jnp.pad(w, ((0, 0), (p, 3 - p), (0, 0), (0, 0))) for p in range(4)], axis=3)
    w = w.reshape(3, 6 * HID, 4 * HID)
    w_a, w_b, w_c = w[:, 0:768, 0:256], w[:, 128:1024, 256:512], w[:, 384:1152, 512:768]
    w = conv_out.transpose(0, 1, 3, 2)
    w = jnp.stack([jnp.pad(w, ((0, 0), (p, 7 - p), (0, 0), (0, 0))) for p in range(8)], axis=3)
    w_out = w.reshape(3, 10 * HID, 8 * CH)
    return [w_in, w_a, w_b, w_c, w_out]


def shards(x_start, noise, fresh, sched, conv_in, conv_mid, conv_out, time_weight):
    column_parts, row_parts = 128 // COLS, 16 // ROWS
    strips = lax.axis_size("rows")
    slot, strip = lax.axis_index("tm"), lax.axis_index("rows")
    column, quarter = slot // row_parts, slot % row_parts

    down, up = [], []
    for c in range(column_parts):
        place = [(c * row_parts + k % row_parts) * strips + k // row_parts for k in range(strips * row_parts)]
        down += list(zip(place[:-1], place[1:]))
        up += list(zip(place[1:], place[:-1]))

    def rim(for_upper, for_lower):
        below = lax.ppermute(for_upper, ("tm", "rows"), up)
        above = lax.ppermute(for_lower, ("tm", "rows"), down)
        return above, below

    strip_up = [(i + 1, i) for i in range(strips - 1)]
    strip_down = [(i, i + 1) for i in range(strips - 1)]
    latent = x_start[0]
    above = lax.ppermute(latent[:, 13:16].astype(BF), "rows", strip_down)
    below = lax.ppermute(latent[:, 0:3].astype(BF), "rows", strip_up)

    z = noise[0, 0].transpose(1, 2, 0)
    high = lax.reduce_precision(z, 8, 7)
    low_half = (z - high).astype(BF).reshape(16, column_parts, COLS * CH)
    high = jnp.pad(high.astype(BF), ((0, 0), (9, 9), (0, 0))).reshape(16, 146 * CH)
    parts = []
    for c in range(column_parts):
        parts.append(
            jnp.concatenate(
                [high[:, 256 * c : 256 * c + 544], low_half[:, c], jnp.zeros((16, 224), BF)], axis=-1
            )
        )
    sent = jnp.stack(parts).reshape(SLOTS, ROWS * 8, 128)
    got = lax.all_to_all(sent, "tm", 0, 0, tiled=True)
    got = got.reshape(SLOTS, ROWS, 1024).transpose(1, 0, 2)
    z9 = jnp.pad(got[:, :, 0:544].astype(F32), ((0, 0), (0, 0), (0, 96)))
    z9 = z9 + jnp.pad(got[:, :, 544:800].astype(F32), ((0, 0), (0, 0), (144, 240)))

    weights = banded_weights(conv_in, conv_mid, conv_out)
    values, embedding = plan_values(sched, time_weight, HID)

    def coefs(r):
        mine = values[:, RETIRE * r : RETIRE * r + SLOTS]
        table = jnp.broadcast_to(mine[:, :, None], (3, SLOTS, 128))
        emb = jnp.tile(embedding[RETIRE * r : RETIRE * r + SLOTS], (1, 4))
        return table, emb.reshape(SLOTS, 3, 256).transpose(1, 0, 2)

    i, j = jnp.arange(SLOTS)[None], jnp.arange(SLOTS)[:, None]
    low = (i < j).astype(F32)
    moved = jnp.where(j < SLOTS - RETIRE, j + RETIRE, j)
    low_2 = jnp.concatenate([low, (i < moved).astype(F32)])

    flags = jnp.stack(
        [
            column == 0,
            column == column_parts - 1,
            (strip == 0) & (quarter == 0),
            (strip == strips - 1) & (quarter == row_parts - 1),
        ]
    ).astype(jnp.int32)

    f = fresh[:, 0].transpose(2, 0, 3, 1)
    f = jnp.pad(f, ((0, 0), (0, 0), (3, 5), (0, 0))).reshape(16, RETIRE, 136 * CH)
    f = lax.dynamic_slice(f, (quarter * ROWS, 0, column * 256), (ROWS, RETIRE, 384))
    lane = jnp.arange(384)
    f = jnp.where(lane < 352, f, 0.0)
    z3 = jnp.concatenate([z9[:, RETIRE:, 96:480], f], axis=1)

    x = jnp.concatenate([above.astype(F32), latent, below.astype(F32)], axis=1)
    x = jnp.pad(x.transpose(1, 2, 0), ((0, 0), (12, 20), (0, 0))).reshape(22, 160 * CH)
    x = lax.dynamic_slice(x, (quarter * ROWS, column * 256), (ROWS + 6, 768))
    x = jnp.broadcast_to(x[:, None], (ROWS + 6, 8, 768))

    table, emb = coefs(0)
    s1, to_upper, to_lower = sweep_call(0, MERGE, flags, [x, z9, table, emb, *weights, low])
    above, below = rim(to_upper, to_lower)
    first_out, s2, to_upper, to_lower = sweep_call(
        1, MERGE, flags, [above, s1, below, x, z9, table, emb, *weights, low_2]
    )
    above, below = rim(to_upper, to_lower)
    table, emb = coefs(1)
    s3, to_upper, to_lower = sweep_call(
        2, MERGE, flags, [above, s2, below, z3, table, emb, *weights, low]
    )
    above, below = rim(to_upper, to_lower)
    (second_out,) = sweep_call(
        3, MERGE, flags, [above, s3, below, s2, z3, table, emb, *weights, low]
    )
    out = jnp.stack([first_out, second_out]).transpose(2, 0, 1, 3).reshape(SLOTS, 16, 128)
    out = lax.all_to_all(out, "tm", 0, 0, tiled=True)
    out = out.reshape(column_parts, row_parts, 2, ROWS, COLS, CH).transpose(2, 5, 1, 3, 0, 4)
    return out.reshape(2, 1, 1, CH, 16, 128)


MERGE = 2


def solution(mesh):
    placed = (
        P(None, None, "rows", None),
        P("tm", None, None, "rows", None),
        P(None, None, None, "rows", None),
        P(),
        P(),
        P(),
        P(),
        P(),
    )
    return jax.shard_map(
        shards,
        mesh=mesh,
        in_specs=placed,
        out_specs=P(None, "tm", None, None, "rows", None),
        check_vma=False,
    )
```

```python
import functools
import jax
import jax.numpy as jnp
from jax import lax
from jax.experimental import pallas as pl
from jax.experimental.pallas import tpu as pltpu
from jax.sharding import PartitionSpec as P

STEPS = 1000
RETIRE = 5
SLOTS = 32
CH = 16
HID = 192
ROWS = 4
COLS = 16
STEP = 3 * CH
BF = jnp.bfloat16
F32 = jnp.float32


WEIGHTS = ("w_in", "w_a", "w_b", "w_c", "w_out", "coef", "emb", "low")
OPERANDS = (
    ("x", "z") + WEIGHTS,
    ("above", "state", "below", "x", "z") + WEIGHTS,
    ("above", "state", "below", "z") + WEIGHTS,
    ("above", "state", "below", "old", "z") + WEIGHTS,
)


def silu(v):
    half = 0.5 * v
    return half + half * jnp.tanh(half)


def sweep_body(sweep, merge, flags, *refs):
    extra = (9, 6, 3, 0)[sweep]
    out_cols = COLS + 2 * extra
    mid_cols, first_cols = out_cols + 2, out_cols + 4
    lanes = -(-out_cols * CH // 128) * 128
    groups_1 = -(-first_cols // 4)
    names = OPERANDS[sweep]
    count = len(names)
    outs = refs[count : -count - 4]
    held = refs[-count - 4 : -4]
    hs, f1, f2, sem = refs[-4:]
    pending = {
        name: pltpu.make_async_copy(refs[i], held[i], sem.at[i]) for i, name in enumerate(names)
    }
    for copy in pending.values():
        copy.start()

    def fetch(*wanted):
        for name in wanted:
            if name in pending:
                pending.pop(name).wait()

    have = dict(zip(names, held))
    x_ref, u_ref, s_ref, d_ref = (have.get(n) for n in ("x", "above", "state", "below"))
    old_ref, z_ref, coef, emb = (have.get(n) for n in ("old", "z", "coef", "emb"))
    w_in, w_a, w_b, w_c, w_out = (have[n] for n in ("w_in", "w_a", "w_b", "w_c", "w_out"))
    low = have["low"]
    outs = list(outs)
    traj_out = outs.pop(0) if sweep in (1, 3) else None
    if sweep < 3:
        state_out, up_out, down_out = outs
    batch = hs.shape[2]

    fetch(*(("x",) if sweep == 0 else ("above", "state", "below")))
    for y in range(ROWS + 6):
        if sweep == 0:
            row = jnp.concatenate([x_ref[y]] * 2, axis=0).astype(BF)
        elif y < 3:
            row = u_ref[y]
        elif y < 3 + ROWS:
            row = s_ref[y - 3].astype(BF)
        else:
            row = d_ref[y - 3 - ROWS]
        for g in range(groups_1):
            hs[g, y] = row[:, 64 * g : 64 * g + 128]

    rows_1 = (ROWS + 4) * batch

    def stage_1(gs):
        lhs = [
            jnp.concatenate([hs[g, a : a + ROWS + 4] for a in range(3)], axis=-1).reshape(rows_1, 384)
            for g in gs
        ]
        lhs = jnp.concatenate(lhs, axis=0) if len(lhs) > 1 else lhs[0]
        for ph in range(3):
            total = jnp.dot(lhs, w_in[ph], preferred_element_type=F32)
            for i, g in enumerate(gs):
                acc = total[i * rows_1 : (i + 1) * rows_1].reshape(ROWS + 4, batch, 256)
                if batch < SLOTS:
                    acc = jnp.concatenate([acc] * (SLOTS // batch), axis=1)
                acc = silu(acc + emb[sweep // 2, ph][None])
                f1[:, :, pl.ds(aligned(g, 256 * ph), 256)] = acc.astype(BF)

    def aligned(g, off):
        at = 768 * g + off
        return at if isinstance(g, int) else pl.multiple_of(at, 128)

    def over(count, size, stage):
        def many(i, _):
            stage([i * size + k for k in range(size)])
            return 0

        if count // size > 1:
            lax.fori_loop(0, count // size, many, 0)
        else:
            stage(list(range(size)))
        if count % size:
            stage(list(range(count - count % size, count)))

    fetch("w_in", "emb")
    over(groups_1, min(merge[0], groups_1), stage_1)

    def clear(ref, ahead, height, top, bottom):
        width = ref.shape[2]

        @pl.when(flags[0] == 1)
        def _():
            ref[:, :, 0 : ahead * HID] = jnp.zeros((height, SLOTS, ahead * HID), BF)

        @pl.when(flags[1] == 1)
        def _():
            ref[:, :, (ahead + COLS) * HID :] = jnp.zeros(
                (height, SLOTS, width - (ahead + COLS) * HID), BF
            )

        @pl.when(flags[2] == 1)
        def _():
            ref[0:top] = jnp.zeros((top, SLOTS, width), BF)

        @pl.when(flags[3] == 1)
        def _():
            ref[height - bottom :] = jnp.zeros((bottom, SLOTS, width), BF)

    clear(f1, extra + 2, ROWS + 4, 2, 2)

    mid_rows = ROWS + 2

    def window(g, off, length):
        at = aligned(g, off)
        part = [f1[a : a + mid_rows, :, pl.ds(at, length)] for a in range(3)]
        return jnp.concatenate(part, axis=-1).reshape(mid_rows * SLOTS, 3 * length)

    def put(g, off, acc):
        at = aligned(g, off)
        size = acc.shape[-1]
        f2[:, :, pl.ds(at, size)] = silu(acc).astype(BF).reshape(mid_rows, SLOTS, size)

    groups_2 = mid_cols // 4
    rows_2 = mid_rows * SLOTS

    def stage_2(gs):
        for off, length, shift, w in ((0, 768, 0, w_a), (128, 896, 256, w_b), (384, 768, 512, w_c)):
            lhs = [window(g, off, length) for g in gs]
            lhs = jnp.concatenate(lhs, axis=0) if len(lhs) > 1 else lhs[0]
            acc = jnp.dot(lhs, w[...].reshape(3 * length, 256), preferred_element_type=F32)
            for i, g in enumerate(gs):
                put(g, shift, acc[i * rows_2 : (i + 1) * rows_2])

    fetch("w_a", "w_b", "w_c")
    over(groups_2, min(merge[1], groups_2), stage_2)
    if mid_cols % 4:
        g = groups_2
        acc = jnp.dot(
            window(g, 0, 768), w_a[...].reshape(2304, 256), preferred_element_type=F32
        )
        put(g, 0, acc)
        w = jnp.concatenate([w_b[a, 0:640, 0:128] for a in range(3)], axis=0)
        put(g, 256, jnp.dot(window(g, 128, 640), w, preferred_element_type=F32))
    clear(f2, extra + 1, mid_rows, 1, 1)

    fetch(*list(pending))
    full = out_cols // 8
    lhs = [
        jnp.concatenate([f2[a : a + ROWS, :, 1536 * n : 1536 * n + 1920] for a in range(3)], axis=-1)
        .reshape(ROWS * SLOTS, 5760)
        for n in range(full)
    ]
    lhs = jnp.concatenate(lhs, axis=0)
    acc = jnp.dot(lhs, w_out[...].reshape(5760, 128), preferred_element_type=F32)
    acc = acc.reshape(full, ROWS, SLOTS, 128)
    pieces = [acc[n] for n in range(full)]
    left = out_cols - 8 * full
    if left:
        k = (left + 2) * HID
        at = 1536 * full
        lhs = jnp.concatenate([f2[a : a + ROWS, :, at : at + k] for a in range(3)], axis=-1)
        w = jnp.concatenate([w_out[a, 0:k] for a in range(3)], axis=0)
        acc = jnp.dot(lhs.reshape(ROWS * SLOTS, 3 * k), w, preferred_element_type=F32)
        pieces.append(acc.reshape(ROWS, SLOTS, 128))
    predicted = jnp.concatenate(pieces, axis=-1)

    keep, predict, spread = (coef[sweep // 2, k, :, 0:1] for k in range(3))
    z_at = STEP if sweep in (1, 3) else 0
    where = lax.broadcasted_iota(jnp.int32, (1, lanes), 1)
    low_lane = jnp.where(flags[0] == 1, extra * CH, 0)
    high_lane = jnp.where(flags[1] == 1, (extra + COLS) * CH, lanes)
    inside = jnp.where((where >= low_lane) & (where < high_lane), 1.0, 0.0).astype(F32)
    changes = []
    for y in range(ROWS):
        if sweep == 0:
            now = jnp.concatenate([x_ref[y + 3, :, STEP : STEP + lanes]] * 4, axis=0)
        else:
            now = s_ref[y, :, STEP : STEP + lanes]
        z = z_ref[y, :, z_at : z_at + lanes]
        changes.append(keep * now + predict * predicted[y] + spread * z)
    change = jnp.concatenate(changes, axis=-1)
    total = jnp.dot(low[...], change, preferred_element_type=F32, precision=lax.Precision.HIGHEST)
    for y in range(ROWS):
        if sweep == 0:
            base = x_ref[y + 3, 0:1, STEP : STEP + lanes]
        elif sweep == 1:
            base = x_ref[y + 3, 0:1, 2 * STEP : 2 * STEP + lanes]
        elif sweep == 2:
            base = s_ref[y, 0:1, STEP : STEP + lanes]
        else:
            base = old_ref[y, 0:1, 2 * STEP : 2 * STEP + lanes]
        state = base + total[0:SLOTS, y * lanes : (y + 1) * lanes]
        if sweep == 1:
            traj_out[y] = state[:, 2 * STEP : 2 * STEP + COLS * CH]
            state = base + total[SLOTS:, y * lanes : (y + 1) * lanes]
        if sweep == 3:
            traj_out[y] = state
        else:
            state = state * inside
            state_out[y] = state
            if y < 3:
                up_out[y] = state.astype(BF)
            if y > 0:
                down_out[y - 1] = state.astype(BF)


def sweep_call(sweep, merge, flags, args):
    extra = (9, 6, 3, 0)[sweep]
    out_cols = COLS + 2 * extra
    lanes = -(-out_cols * CH // 128) * 128
    groups_1 = -(-(out_cols + 4) // 4)
    groups_2 = (out_cols + 2) // 4
    f1_lanes = max(groups_1 * 768, (groups_2 - 1) * 768 + 1152)
    shapes = []
    if sweep in (1, 3):
        shapes.append(jax.ShapeDtypeStruct((ROWS, SLOTS, COLS * CH), F32))
    if sweep < 3:
        shapes.append(jax.ShapeDtypeStruct((ROWS, SLOTS, lanes), F32))
        shapes += [jax.ShapeDtypeStruct((3, SLOTS, lanes), BF)] * 2
    operands = [args[name] for name in OPERANDS[sweep]]
    vmem = pl.BlockSpec(memory_space=pltpu.VMEM)
    return pl.pallas_call(
        functools.partial(sweep_body, sweep, merge),
        out_shape=tuple(shapes),
        in_specs=[pl.BlockSpec(memory_space=pltpu.SMEM)]
        + [pl.BlockSpec(memory_space=pl.ANY)] * len(operands),
        out_specs=tuple([vmem] * len(shapes)),
        scratch_shapes=[pltpu.VMEM(o.shape, o.dtype) for o in operands]
        + [
            pltpu.VMEM((groups_1, ROWS + 6, 16 if sweep == 0 else SLOTS, 128), BF),
            pltpu.VMEM((ROWS + 4, SLOTS, f1_lanes), BF),
            pltpu.VMEM((ROWS + 2, SLOTS, (out_cols + 2) * HID), BF),
            pltpu.SemaphoreType.DMA((len(operands),)),
        ],
        name=f"sweep{sweep}",
    )(flags, *operands)


def prepare_body(now_ref, after_ref, in_ref, mid_ref, out_ref, time_ref, w_in, w_a, w_b, w_c, w_out, table, emb):
    w_in[...] = jnp.zeros_like(w_in)
    for ref in (w_a, w_b, w_c):
        ref[...] = jnp.zeros_like(ref)
    spots = ((w_a, 0, 768, 0), (w_b, 128, 896, 256), (w_c, 384, 768, 512))
    for a in range(3):
        for b in range(3):
            tap = in_ref[a, b]
            for p in range(4):
                row = a * 128 + (p + b) * CH
                for ph in range(3):
                    lo, hi = max(HID * p, 256 * ph), min(HID * (p + 1), 256 * (ph + 1))
                    if lo < hi:
                        w_in[ph, row : row + CH, lo - 256 * ph : hi - 256 * ph] = tap[:, lo - HID * p : hi - HID * p]
            tap = mid_ref[a, b].astype(F32).T.astype(BF)
            for p in range(4):
                row = (p + b) * HID
                for ref, start, length, lane in spots:
                    lo, hi = max(HID * p, lane), min(HID * (p + 1), lane + 256)
                    top, end = max(row, start), min(row + HID, start + length)
                    if lo < hi and top < end:
                        ref[a, top - start : end - start, lo - lane : hi - lane] = tap[
                            top - row : end - row, lo - HID * p : hi - HID * p
                        ]
    lane = lax.broadcasted_iota(jnp.int32, (1, 128), 1)
    spread_out = (lax.broadcasted_iota(jnp.int32, (CH, 128), 1) % CH == lax.broadcasted_iota(jnp.int32, (CH, 128), 0))
    spread_out = jnp.where(spread_out, 1.0, 0.0).astype(BF)
    for a in range(3):
        taps = [jnp.dot(out_ref[a, b], spread_out, preferred_element_type=F32) for b in range(3)]
        for x in range(10):
            block = jnp.zeros((HID, 128), F32)
            for b in range(3):
                if 0 <= x - b < 8:
                    at = jnp.where(lane // CH == x - b, 1.0, 0.0)
                    block = block + taps[b] * at
            w_out[a, HID * x : HID * (x + 1)] = block.astype(BF)

    now, after = now_ref[...], after_ref[...]
    step = lax.broadcasted_iota(jnp.int32, (1, 1024), 1)
    betas = 0.0001 + (0.02 - 0.0001) * step.astype(F32) / (STEPS - 1)
    logs = jnp.where(step < STEPS, jnp.log(1.0 - betas), 0.0)
    log_now = jnp.sum(jnp.where(step <= now, logs, 0.0), axis=1, keepdims=True)
    log_after = jnp.sum(jnp.where(step <= after, logs, 0.0), axis=1, keepdims=True)
    between = jnp.where(step <= now, logs, 0.0) - jnp.where(step <= after, logs, 0.0)
    retained = jnp.exp(jnp.sum(between, axis=1, keepdims=True))
    bar_now, bar_after = jnp.exp(log_now), jnp.exp(log_after)
    keep = 1.0 / jnp.sqrt(retained) - 1.0
    predict = -(1.0 - retained) / (jnp.sqrt(1.0 - bar_now) * jnp.sqrt(retained))
    spread = jnp.sqrt((1.0 - bar_after) / (1.0 - bar_now) * (1.0 - retained))
    half = HID // 2
    freqs = jnp.exp(
        -9.210340371976184 * lax.broadcasted_iota(jnp.int32, (1, half), 1).astype(F32) / half
    )
    angles = now.astype(F32) * freqs
    features = jnp.concatenate([jnp.sin(angles), jnp.cos(angles)], axis=-1)
    embedding = jnp.dot(
        features, time_ref[...].astype(F32), preferred_element_type=F32, precision=lax.Precision.HIGHEST
    )
    wide = jnp.concatenate([embedding] * 4, axis=-1)
    for r in range(2):
        rows = slice(RETIRE * r, RETIRE * r + SLOTS)
        for k, value in enumerate((keep, predict, spread)):
            table[r, k] = jnp.broadcast_to(value, (value.shape[0], 128))[rows]
        for ph in range(3):
            emb[r, ph] = wide[rows, 256 * ph : 256 * ph + 256]


def prepare(sched, conv_in, conv_mid, conv_out, time_weight):
    now = jnp.pad(sched[:37], (0, 3), constant_values=999)[:, None]
    after = jnp.pad(sched[1:], (0, 3), constant_values=998)[:, None]
    shapes = [
        jax.ShapeDtypeStruct(s, d)
        for s, d in (
            ((3, 384, 256), BF),
            ((3, 768, 256), BF),
            ((3, 896, 256), BF),
            ((3, 768, 256), BF),
            ((3, 1920, 128), BF),
            ((2, 3, SLOTS, 128), F32),
            ((2, 3, SLOTS, 256), F32),
        )
    ]
    vmem = pl.BlockSpec(memory_space=pltpu.VMEM)
    return pl.pallas_call(
        prepare_body,
        out_shape=tuple(shapes),
        in_specs=[vmem] * 6,
        out_specs=tuple([vmem] * len(shapes)),
        name="prepare",
    )(now, after, conv_in.transpose(0, 1, 3, 2), conv_mid, conv_out.transpose(0, 1, 3, 2), time_weight)


def shards(x_start, noise, fresh, sched, conv_in, conv_mid, conv_out, time_weight):
    column_parts, row_parts = 128 // COLS, 16 // ROWS
    strips = lax.axis_size("rows")
    slot, strip = lax.axis_index("tm"), lax.axis_index("rows")
    column, quarter = slot // row_parts, slot % row_parts

    down, up = [], []
    for c in range(column_parts):
        place = [(c * row_parts + k % row_parts) * strips + k // row_parts for k in range(strips * row_parts)]
        down += list(zip(place[:-1], place[1:]))
        up += list(zip(place[1:], place[:-1]))

    def rim(for_upper, for_lower):
        below = lax.ppermute(for_upper, ("tm", "rows"), up)
        above = lax.ppermute(for_lower, ("tm", "rows"), down)
        return above, below

    strip_up = [(i + 1, i) for i in range(strips - 1)]
    strip_down = [(i, i + 1) for i in range(strips - 1)]
    latent = x_start[0]
    above = lax.ppermute(latent[:, 13:16].astype(BF), "rows", strip_down)
    below = lax.ppermute(latent[:, 0:3].astype(BF), "rows", strip_up)

    z = noise[0, 0].transpose(1, 2, 0)
    high = lax.reduce_precision(z, 8, 7)
    low_half = (z - high).astype(BF).reshape(16, column_parts, COLS * CH)
    high = jnp.pad(high.astype(BF), ((0, 0), (9, 9), (0, 0))).reshape(16, 146 * CH)
    parts = []
    for c in range(column_parts):
        parts.append(
            jnp.concatenate(
                [high[:, 256 * c : 256 * c + 544], low_half[:, c], jnp.zeros((16, 224), BF)], axis=-1
            )
        )
    sent = jnp.stack(parts).reshape(SLOTS, ROWS * 8, 128)
    got = lax.all_to_all(sent, "tm", 0, 0, tiled=True)
    got = got.reshape(SLOTS, ROWS, 1024).transpose(1, 0, 2)
    z9 = jnp.pad(got[:, :, 0:544].astype(F32), ((0, 0), (0, 0), (0, 96)))
    z9 = z9 + jnp.pad(got[:, :, 544:800].astype(F32), ((0, 0), (0, 0), (144, 240)))

    *weights, table, emb = prepare(sched, conv_in, conv_mid, conv_out, time_weight)

    i, j = jnp.arange(SLOTS)[None], jnp.arange(SLOTS)[:, None]
    low = (i < j).astype(F32)
    moved = jnp.where(j < SLOTS - RETIRE, j + RETIRE, j)
    low_2 = jnp.concatenate([low, (i < moved).astype(F32)])

    flags = jnp.stack(
        [
            column == 0,
            column == column_parts - 1,
            (strip == 0) & (quarter == 0),
            (strip == strips - 1) & (quarter == row_parts - 1),
        ]
    ).astype(jnp.int32)

    f = jnp.pad(fresh[:, 0], ((0, 0), (0, 0), (0, 0), (3, 5)))
    f = lax.dynamic_slice(f, (0, 0, quarter * ROWS, column * COLS), (RETIRE, CH, ROWS, 24))
    f = f.transpose(2, 0, 3, 1).reshape(ROWS, RETIRE, 384)
    f = jnp.where(jnp.arange(384) < 352, f, 0.0)
    z3 = jnp.concatenate([z9[:, RETIRE:, 96:480], f], axis=1)

    x = jnp.concatenate([above.astype(F32), latent, below.astype(F32)], axis=1)
    x = jnp.pad(x, ((0, 0), (0, 0), (12, 20)))
    x = lax.dynamic_slice(x, (0, quarter * ROWS, column * COLS), (CH, ROWS + 6, 48))
    x = x.transpose(1, 2, 0).reshape(ROWS + 6, 1, 768)
    x = jnp.broadcast_to(x, (ROWS + 6, 8, 768))

    args = dict(zip(("w_in", "w_a", "w_b", "w_c", "w_out"), weights), coef=table, emb=emb, x=x, z=z9, low=low)
    s1, to_upper, to_lower = sweep_call(0, MERGE[0], flags, args)
    above, below = rim(to_upper, to_lower)
    args.update(above=above, state=s1, below=below, low=low_2)
    first_out, s2, to_upper, to_lower = sweep_call(1, MERGE[1], flags, args)
    above, below = rim(to_upper, to_lower)
    args.update(above=above, state=s2, below=below, low=low, z=z3)
    s3, to_upper, to_lower = sweep_call(2, MERGE[2], flags, args)
    above, below = rim(to_upper, to_lower)
    args.update(above=above, state=s3, below=below, old=s2)
    (second_out,) = sweep_call(3, MERGE[3], flags, args)
    out = jnp.stack([first_out, second_out]).transpose(2, 0, 1, 3).reshape(SLOTS, 16, 128)
    out = lax.all_to_all(out, "tm", 0, 0, tiled=True)
    out = out.reshape(column_parts, row_parts, 2, ROWS, COLS, CH).transpose(2, 5, 1, 3, 0, 4)
    return out.reshape(2, 1, 1, CH, 16, 128)


MERGE = ((2, 4), (2, 4), (2, 4), (1, 3))


def solution(mesh):
    placed = (
        P(None, None, "rows", None),
        P("tm", None, None, "rows", None),
        P(None, None, None, "rows", None),
        P(),
        P(),
        P(),
        P(),
        P(),
    )
    return jax.shard_map(
        shards,
        mesh=mesh,
        in_specs=placed,
        out_specs=P(None, "tm", None, None, "rows", None),
        check_vma=False,
    )
```

```python
import functools
import jax
import jax.numpy as jnp
from jax import lax
from jax.experimental import pallas as pl
from jax.experimental.pallas import tpu as pltpu
from jax.sharding import PartitionSpec as P

STEPS = 1000
RETIRE = 5
SLOTS = 32
CH = 16
HID = 192
ROWS = 4
COLS = 16
STEP = 3 * CH
BF = jnp.bfloat16
F32 = jnp.float32


WEIGHTS = ("w_in", "w_a", "w_b", "w_c", "w_out", "coef", "emb", "low")
OPERANDS = (
    ("x", "z") + WEIGHTS,
    ("above", "state", "below", "x", "z") + WEIGHTS,
    ("above", "state", "below", "z") + WEIGHTS,
    ("above", "state", "below", "old", "z") + WEIGHTS,
)


def silu(v):
    half = 0.5 * v
    return half + half * jnp.tanh(half)


def sweep_body(sweep, merge, flags, *refs):
    extra = (9, 6, 3, 0)[sweep]
    out_cols = COLS + 2 * extra
    mid_cols, first_cols = out_cols + 2, out_cols + 4
    lanes = -(-out_cols * CH // 128) * 128
    groups_1 = -(-first_cols // 4)
    names = OPERANDS[sweep]
    count = len(names)
    outs = refs[count : -count - 4]
    held = refs[-count - 4 : -4]
    hs, f1, f2, sem = refs[-4:]
    pending = {
        name: pltpu.make_async_copy(refs[i], held[i], sem.at[i]) for i, name in enumerate(names)
    }
    early = ("x",) if sweep == 0 else ("above", "state", "below")
    for name in early + ("w_in", "emb"):
        pending[name].start()

    def fetch(*wanted):
        for name in wanted:
            if name in pending:
                pending.pop(name).wait()

    have = dict(zip(names, held))
    x_ref, u_ref, s_ref, d_ref = (have.get(n) for n in ("x", "above", "state", "below"))
    old_ref, z_ref, coef, emb = (have.get(n) for n in ("old", "z", "coef", "emb"))
    w_in, w_a, w_b, w_c, w_out = (have[n] for n in ("w_in", "w_a", "w_b", "w_c", "w_out"))
    low = have["low"]
    outs = list(outs)
    traj_out = outs.pop(0) if sweep in (1, 3) else None
    if sweep < 3:
        state_out, up_out, down_out = outs
    batch = hs.shape[2]

    fetch(*early)
    for y in range(ROWS + 6):
        if sweep == 0:
            row = jnp.concatenate([x_ref[y]] * 2, axis=0).astype(BF)
        elif y < 3:
            row = u_ref[y]
        elif y < 3 + ROWS:
            row = s_ref[y - 3].astype(BF)
        else:
            row = d_ref[y - 3 - ROWS]
        for g in range(groups_1):
            hs[g, y] = row[:, 64 * g : 64 * g + 128]

    rows_1 = (ROWS + 4) * batch

    def stage_1(gs):
        lhs = [
            jnp.concatenate([hs[g, a : a + ROWS + 4] for a in range(3)], axis=-1).reshape(rows_1, 384)
            for g in gs
        ]
        lhs = jnp.concatenate(lhs, axis=0) if len(lhs) > 1 else lhs[0]
        for ph in range(3):
            total = jnp.dot(lhs, w_in[ph], preferred_element_type=F32)
            for i, g in enumerate(gs):
                acc = total[i * rows_1 : (i + 1) * rows_1].reshape(ROWS + 4, batch, 256)
                if batch < SLOTS:
                    acc = jnp.concatenate([acc] * (SLOTS // batch), axis=1)
                acc = silu(acc + emb[sweep // 2, ph][None])
                f1[:, :, pl.ds(aligned(g, 256 * ph), 256)] = acc.astype(BF)

    def aligned(g, off):
        at = 768 * g + off
        return at if isinstance(g, int) else pl.multiple_of(at, 128)

    def over(count, size, stage):
        def many(i, _):
            stage([i * size + k for k in range(size)])
            return 0

        if count // size > 1:
            lax.fori_loop(0, count // size, many, 0)
        else:
            stage(list(range(size)))
        if count % size:
            stage(list(range(count - count % size, count)))

    fetch("w_in", "emb")
    for name in ("w_a", "w_b", "w_c", "w_out", "z", "x", "old", "coef", "low"):
        if name in pending:
            pending[name].start()
    over(groups_1, min(merge[0], groups_1), stage_1)

    def clear(ref, ahead, height, top, bottom):
        width = ref.shape[2]

        @pl.when(flags[0] == 1)
        def _():
            ref[:, :, 0 : ahead * HID] = jnp.zeros((height, SLOTS, ahead * HID), BF)

        @pl.when(flags[1] == 1)
        def _():
            ref[:, :, (ahead + COLS) * HID :] = jnp.zeros(
                (height, SLOTS, width - (ahead + COLS) * HID), BF
            )

        @pl.when(flags[2] == 1)
        def _():
            ref[0:top] = jnp.zeros((top, SLOTS, width), BF)

        @pl.when(flags[3] == 1)
        def _():
            ref[height - bottom :] = jnp.zeros((bottom, SLOTS, width), BF)

    clear(f1, extra + 2, ROWS + 4, 2, 2)

    mid_rows = ROWS + 2

    def window(g, off, length):
        at = aligned(g, off)
        part = [f1[a : a + mid_rows, :, pl.ds(at, length)] for a in range(3)]
        return jnp.concatenate(part, axis=-1).reshape(mid_rows * SLOTS, 3 * length)

    def put(g, off, acc):
        at = aligned(g, off)
        size = acc.shape[-1]
        f2[:, :, pl.ds(at, size)] = silu(acc).astype(BF).reshape(mid_rows, SLOTS, size)

    groups_2 = mid_cols // 4
    rows_2 = mid_rows * SLOTS

    def stage_2(gs):
        for off, length, shift, w in ((0, 768, 0, w_a), (128, 896, 256, w_b), (384, 768, 512, w_c)):
            lhs = [window(g, off, length) for g in gs]
            lhs = jnp.concatenate(lhs, axis=0) if len(lhs) > 1 else lhs[0]
            acc = jnp.dot(lhs, w[...].reshape(3 * length, 256), preferred_element_type=F32)
            for i, g in enumerate(gs):
                put(g, shift, acc[i * rows_2 : (i + 1) * rows_2])

    fetch("w_a", "w_b", "w_c")
    over(groups_2, min(merge[1], groups_2), stage_2)
    if mid_cols % 4:
        g = groups_2
        acc = jnp.dot(
            window(g, 0, 768), w_a[...].reshape(2304, 256), preferred_element_type=F32
        )
        put(g, 0, acc)
        w = jnp.concatenate([w_b[a, 0:640, 0:128] for a in range(3)], axis=0)
        put(g, 256, jnp.dot(window(g, 128, 640), w, preferred_element_type=F32))
    clear(f2, extra + 1, mid_rows, 1, 1)

    fetch(*list(pending))
    full = out_cols // 8
    lhs = [
        jnp.concatenate([f2[a : a + ROWS, :, 1536 * n : 1536 * n + 1920] for a in range(3)], axis=-1)
        .reshape(ROWS * SLOTS, 5760)
        for n in range(full)
    ]
    lhs = jnp.concatenate(lhs, axis=0)
    acc = jnp.dot(lhs, w_out[...].reshape(5760, 128), preferred_element_type=F32)
    acc = acc.reshape(full, ROWS, SLOTS, 128)
    pieces = [acc[n] for n in range(full)]
    left = out_cols - 8 * full
    if left:
        k = (left + 2) * HID
        at = 1536 * full
        lhs = jnp.concatenate([f2[a : a + ROWS, :, at : at + k] for a in range(3)], axis=-1)
        w = jnp.concatenate([w_out[a, 0:k] for a in range(3)], axis=0)
        acc = jnp.dot(lhs.reshape(ROWS * SLOTS, 3 * k), w, preferred_element_type=F32)
        pieces.append(acc.reshape(ROWS, SLOTS, 128))
    predicted = jnp.concatenate(pieces, axis=-1)

    keep, predict, spread = (coef[sweep // 2, k, :, 0:1] for k in range(3))
    z_at = STEP if sweep in (1, 3) else 0
    where = lax.broadcasted_iota(jnp.int32, (1, lanes), 1)
    low_lane = jnp.where(flags[0] == 1, extra * CH, 0)
    high_lane = jnp.where(flags[1] == 1, (extra + COLS) * CH, lanes)
    inside = jnp.where((where >= low_lane) & (where < high_lane), 1.0, 0.0).astype(F32)
    changes = []
    for y in range(ROWS):
        if sweep == 0:
            now = jnp.concatenate([x_ref[y + 3, :, STEP : STEP + lanes]] * 4, axis=0)
        else:
            now = s_ref[y, :, STEP : STEP + lanes]
        z = z_ref[y, :, z_at : z_at + lanes]
        changes.append(keep * now + predict * predicted[y] + spread * z)
    change = jnp.concatenate(changes, axis=-1)
    total = jnp.dot(low[...], change, preferred_element_type=F32, precision=lax.Precision.HIGHEST)
    for y in range(ROWS):
        if sweep == 0:
            base = x_ref[y + 3, 0:1, STEP : STEP + lanes]
        elif sweep == 1:
            base = x_ref[y + 3, 0:1, 2 * STEP : 2 * STEP + lanes]
        elif sweep == 2:
            base = s_ref[y, 0:1, STEP : STEP + lanes]
        else:
            base = old_ref[y, 0:1, 2 * STEP : 2 * STEP + lanes]
        state = base + total[0:SLOTS, y * lanes : (y + 1) * lanes]
        if sweep == 1:
            traj_out[y] = state[:, 2 * STEP : 2 * STEP + COLS * CH]
            state = base + total[SLOTS:, y * lanes : (y + 1) * lanes]
        if sweep == 3:
            traj_out[y] = state
        else:
            state = state * inside
            state_out[y] = state
            if y < 3:
                up_out[y] = state.astype(BF)
            if y > 0:
                down_out[y - 1] = state.astype(BF)


def sweep_call(sweep, merge, flags, args):
    extra = (9, 6, 3, 0)[sweep]
    out_cols = COLS + 2 * extra
    lanes = -(-out_cols * CH // 128) * 128
    groups_1 = -(-(out_cols + 4) // 4)
    groups_2 = (out_cols + 2) // 4
    f1_lanes = max(groups_1 * 768, (groups_2 - 1) * 768 + 1152)
    shapes = []
    if sweep in (1, 3):
        shapes.append(jax.ShapeDtypeStruct((ROWS, SLOTS, COLS * CH), F32))
    if sweep < 3:
        shapes.append(jax.ShapeDtypeStruct((ROWS, SLOTS, lanes), F32))
        shapes += [jax.ShapeDtypeStruct((3, SLOTS, lanes), BF)] * 2
    operands = [args[name] for name in OPERANDS[sweep]]
    vmem = pl.BlockSpec(memory_space=pltpu.VMEM)
    return pl.pallas_call(
        functools.partial(sweep_body, sweep, merge),
        out_shape=tuple(shapes),
        in_specs=[pl.BlockSpec(memory_space=pltpu.SMEM)]
        + [pl.BlockSpec(memory_space=pl.ANY)] * len(operands),
        out_specs=tuple([vmem] * len(shapes)),
        scratch_shapes=[pltpu.VMEM(o.shape, o.dtype) for o in operands]
        + [
            pltpu.VMEM((groups_1, ROWS + 6, 16 if sweep == 0 else SLOTS, 128), BF),
            pltpu.VMEM((ROWS + 4, SLOTS, f1_lanes), BF),
            pltpu.VMEM((ROWS + 2, SLOTS, (out_cols + 2) * HID), BF),
            pltpu.SemaphoreType.DMA((len(operands),)),
        ],
        name=f"sweep{sweep}",
    )(flags, *operands)


def prepare_body(plan_ref, in_ref, mid_ref, out_ref, time_ref, w_in, w_a, w_b, w_c, w_out, table, emb):
    w_in[...] = jnp.zeros_like(w_in)
    for ref in (w_a, w_b, w_c):
        ref[...] = jnp.zeros_like(ref)
    spots = ((w_a, 0, 768, 0), (w_b, 128, 896, 256), (w_c, 384, 768, 512))
    for a in range(3):
        for b in range(3):
            tap = in_ref[a, b]
            for p in range(4):
                row = a * 128 + (p + b) * CH
                for ph in range(3):
                    lo, hi = max(HID * p, 256 * ph), min(HID * (p + 1), 256 * (ph + 1))
                    if lo < hi:
                        w_in[ph, row : row + CH, lo - 256 * ph : hi - 256 * ph] = tap[:, lo - HID * p : hi - HID * p]
            tap = mid_ref[a, b].astype(F32).T.astype(BF)
            for p in range(4):
                row = (p + b) * HID
                for ref, start, length, lane in spots:
                    lo, hi = max(HID * p, lane), min(HID * (p + 1), lane + 256)
                    top, end = max(row, start), min(row + HID, start + length)
                    if lo < hi and top < end:
                        ref[a, top - start : end - start, lo - lane : hi - lane] = tap[
                            top - row : end - row, lo - HID * p : hi - HID * p
                        ]
    lane = lax.broadcasted_iota(jnp.int32, (1, 128), 1)
    spread_out = (lax.broadcasted_iota(jnp.int32, (CH, 128), 1) % CH == lax.broadcasted_iota(jnp.int32, (CH, 128), 0))
    spread_out = jnp.where(spread_out, 1.0, 0.0).astype(BF)
    for a in range(3):
        taps = [jnp.dot(out_ref[a, b], spread_out, preferred_element_type=F32) for b in range(3)]
        for x in range(10):
            block = jnp.zeros((HID, 128), F32)
            for b in range(3):
                if 0 <= x - b < 8:
                    at = jnp.where(lane // CH == x - b, 1.0, 0.0)
                    block = block + taps[b] * at
            w_out[a, HID * x : HID * (x + 1)] = block.astype(BF)

    now, after = plan_ref[:, 0:1], plan_ref[:, 1:2]
    step = lax.broadcasted_iota(jnp.int32, (1, 1024), 1)
    betas = 0.0001 + (0.02 - 0.0001) * step.astype(F32) / (STEPS - 1)
    logs = jnp.where(step < STEPS, jnp.log(1.0 - betas), 0.0)
    log_now = jnp.sum(jnp.where(step <= now, logs, 0.0), axis=1, keepdims=True)
    log_after = jnp.sum(jnp.where(step <= after, logs, 0.0), axis=1, keepdims=True)
    between = jnp.where(step <= now, logs, 0.0) - jnp.where(step <= after, logs, 0.0)
    retained = jnp.exp(jnp.sum(between, axis=1, keepdims=True))
    bar_now, bar_after = jnp.exp(log_now), jnp.exp(log_after)
    keep = 1.0 / jnp.sqrt(retained) - 1.0
    predict = -(1.0 - retained) / (jnp.sqrt(1.0 - bar_now) * jnp.sqrt(retained))
    spread = jnp.sqrt((1.0 - bar_after) / (1.0 - bar_now) * (1.0 - retained))
    half = HID // 2
    freqs = jnp.exp(
        -9.210340371976184 * lax.broadcasted_iota(jnp.int32, (1, half), 1).astype(F32) / half
    )
    angles = now.astype(F32) * freqs
    features = jnp.concatenate([jnp.sin(angles), jnp.cos(angles)], axis=-1)
    embedding = jnp.dot(
        features, time_ref[...].astype(F32), preferred_element_type=F32, precision=lax.Precision.HIGHEST
    )
    wide = jnp.concatenate([embedding] * 4, axis=-1)
    for r in range(2):
        rows = slice(RETIRE * r, RETIRE * r + SLOTS)
        for k, value in enumerate((keep, predict, spread)):
            table[r, k] = jnp.broadcast_to(value, (value.shape[0], 128))[rows]
        for ph in range(3):
            emb[r, ph] = wide[rows, 256 * ph : 256 * ph + 256]


def prepare(sched, conv_in, conv_mid, conv_out, time_weight):
    plan = jnp.pad(jnp.stack([sched[:37], sched[1:]], axis=1), ((0, 3), (0, 0)), mode="edge")
    shapes = [
        jax.ShapeDtypeStruct(s, d)
        for s, d in (
            ((3, 384, 256), BF),
            ((3, 768, 256), BF),
            ((3, 896, 256), BF),
            ((3, 768, 256), BF),
            ((3, 1920, 128), BF),
            ((2, 3, SLOTS, 128), F32),
            ((2, 3, SLOTS, 256), F32),
        )
    ]
    vmem = pl.BlockSpec(memory_space=pltpu.VMEM)
    return pl.pallas_call(
        prepare_body,
        out_shape=tuple(shapes),
        in_specs=[vmem] * 5,
        out_specs=tuple([vmem] * len(shapes)),
        name="prepare",
    )(plan, conv_in.transpose(0, 1, 3, 2), conv_mid, conv_out.transpose(0, 1, 3, 2), time_weight)


def shards(x_start, noise, fresh, sched, conv_in, conv_mid, conv_out, time_weight):
    column_parts, row_parts = 128 // COLS, 16 // ROWS
    strips = lax.axis_size("rows")
    slot, strip = lax.axis_index("tm"), lax.axis_index("rows")
    column, quarter = slot // row_parts, slot % row_parts

    down, up = [], []
    for c in range(column_parts):
        place = [(c * row_parts + k % row_parts) * strips + k // row_parts for k in range(strips * row_parts)]
        down += list(zip(place[:-1], place[1:]))
        up += list(zip(place[1:], place[:-1]))

    def rim(for_upper, for_lower):
        below = lax.ppermute(for_upper, ("tm", "rows"), up)
        above = lax.ppermute(for_lower, ("tm", "rows"), down)
        return above, below

    strip_up = [(i + 1, i) for i in range(strips - 1)]
    strip_down = [(i, i + 1) for i in range(strips - 1)]
    latent = x_start[0]
    above = lax.ppermute(latent[:, 13:16].astype(BF), "rows", strip_down)
    below = lax.ppermute(latent[:, 0:3].astype(BF), "rows", strip_up)

    z = noise[0, 0].transpose(1, 2, 0)
    high = lax.reduce_precision(z, 8, 7)
    low_half = (z - high).astype(BF).reshape(16, column_parts, COLS * CH)
    high = jnp.pad(high.astype(BF), ((0, 0), (9, 9), (0, 0))).reshape(16, 146 * CH)
    parts = []
    for c in range(column_parts):
        parts.append(
            jnp.concatenate(
                [high[:, 256 * c : 256 * c + 544], low_half[:, c], jnp.zeros((16, 224), BF)], axis=-1
            )
        )
    sent = jnp.stack(parts).reshape(SLOTS, ROWS * 8, 128)
    got = lax.all_to_all(sent, "tm", 0, 0, tiled=True)
    got = got.reshape(SLOTS, ROWS, 1024).transpose(1, 0, 2)
    z9 = jnp.pad(got[:, :, 0:544].astype(F32), ((0, 0), (0, 0), (0, 96)))
    z9 = z9 + jnp.pad(got[:, :, 544:800].astype(F32), ((0, 0), (0, 0), (144, 240)))

    *weights, table, emb = prepare(sched, conv_in, conv_mid, conv_out, time_weight)

    i, j = jnp.arange(SLOTS)[None], jnp.arange(SLOTS)[:, None]
    low = (i < j).astype(F32)
    moved = jnp.where(j < SLOTS - RETIRE, j + RETIRE, j)
    low_2 = jnp.concatenate([low, (i < moved).astype(F32)])

    flags = jnp.stack(
        [
            column == 0,
            column == column_parts - 1,
            (strip == 0) & (quarter == 0),
            (strip == strips - 1) & (quarter == row_parts - 1),
        ]
    ).astype(jnp.int32)

    f = jnp.pad(fresh[:, 0], ((0, 0), (0, 0), (0, 0), (3, 5)))
    f = lax.dynamic_slice(f, (0, 0, quarter * ROWS, column * COLS), (RETIRE, CH, ROWS, 24))
    f = f.transpose(2, 0, 3, 1).reshape(ROWS, RETIRE, 384)
    f = jnp.where(jnp.arange(384) < 352, f, 0.0)
    z3 = jnp.concatenate([z9[:, RETIRE:, 96:480], f], axis=1)

    x = jnp.concatenate([above.astype(F32), latent, below.astype(F32)], axis=1)
    x = jnp.pad(x, ((0, 0), (0, 0), (12, 20)))
    x = lax.dynamic_slice(x, (0, quarter * ROWS, column * COLS), (CH, ROWS + 6, 48))
    x = x.transpose(1, 2, 0).reshape(ROWS + 6, 1, 768)
    x = jnp.broadcast_to(x, (ROWS + 6, 8, 768))

    args = dict(zip(("w_in", "w_a", "w_b", "w_c", "w_out"), weights), coef=table, emb=emb, x=x, z=z9, low=low)
    s1, to_upper, to_lower = sweep_call(0, MERGE[0], flags, args)
    above, below = rim(to_upper, to_lower)
    args.update(above=above, state=s1, below=below, low=low_2)
    first_out, s2, to_upper, to_lower = sweep_call(1, MERGE[1], flags, args)
    above, below = rim(to_upper, to_lower)
    args.update(above=above, state=s2, below=below, low=low, z=z3)
    s3, to_upper, to_lower = sweep_call(2, MERGE[2], flags, args)
    above, below = rim(to_upper, to_lower)
    args.update(above=above, state=s3, below=below, old=s2)
    (second_out,) = sweep_call(3, MERGE[3], flags, args)
    out = jnp.stack([first_out, second_out]).transpose(2, 0, 1, 3).reshape(SLOTS, 16, 128)
    out = lax.all_to_all(out, "tm", 0, 0, tiled=True)
    out = out.reshape(column_parts, row_parts, 2, ROWS, COLS, CH).transpose(2, 5, 1, 3, 0, 4)
    return out.reshape(2, 1, 1, CH, 16, 128)


MERGE = ((2, 4), (1, 3), (2, 4), (1, 3))


def solution(mesh):
    placed = (
        P(None, None, "rows", None),
        P("tm", None, None, "rows", None),
        P(None, None, None, "rows", None),
        P(),
        P(),
        P(),
        P(),
        P(),
    )
    return jax.shard_map(
        shards,
        mesh=mesh,
        in_specs=placed,
        out_specs=P(None, "tm", None, None, "rows", None),
        check_vma=False,
    )
```
